32 devices in a mesh: expert: 16 (over z, y, x), shard: 2 (over core).
Axes of the slice: x: 2, y: 2, z: 4, core: 2. Of those that a mesh axis runs over, the one named last changes fastest.
Arguments:
- expert_rows: bfloat16 [16, 1536, 5120], P('expert', None, 'shard'), may hold values from -45 to 45
- sketch: bfloat16 [5120, 256], P('shard'), may hold values from -0.078125 to 0.078125
- permutation: int32 [16, 1536], P('expert'), may hold values from 0 to 1535, each once within a row
- clusters: int32 [16], replicated, may hold values from 0 to 3, as said below
- frequency: int32 [16], replicated, may hold values from 20 to 64
Outputs:
- merged: bfloat16 [16, 1536, 1280], P('expert', None, 'shard')
- basis: float32 [16, 384, 256], P('expert', 'shard')
- coefficients: float32 [16, 256, 1280], P('expert', None, 'shard')
The draws below stay inside these ranges and needn't reach their ends.
Inputs may be any that keep to these rules, and one draw needn't show every extreme that they name: `clusters`: the source experts of merged experts 2 w and 2 w + 1 are exactly the source experts 2 * 4 * w to 2 * 4 * w + 2 * 4 - 1; each merged expert holds 2 to 6 source experts, and some merged expert holds exactly 6.
All inputs are finite; a program needn't handle non-finite values.
Results may differ from the reference program's by a relative error of at most 0.0065.
Values may be sent and summed in bfloat16 or wider, within the bound.
A program may use at most 128 MiB of HBM per device.

```python
import math
import jax
import jax.numpy as jnp
from jax import lax

D = 5120
FF = 1536
RANK = 256
GROUP = 4
CMAX = 6
EXPERTS = 16
N_SHARD = 2


def draw_expert_rows(key, part):
    key_rows, key_cols, key_noise = jax.random.split(key, 3)
    row_scale = jnp.exp(jax.random.uniform(key_rows, (EXPERTS, FF, 1), jnp.float32, -1.2, 1.2))
    col_scale = jnp.exp(jax.random.uniform(key_cols, (EXPERTS, 1, D), jnp.float32, -1.2, 1.2))
    noise_part = jax.random.truncated_normal(key_noise, -4.0, 4.0, (EXPERTS, FF, D), jnp.float32)
    return (row_scale * col_scale * noise_part).astype(jnp.bfloat16)


def draw_clusters(key, part):
    key_size, key_forced, key_order = jax.random.split(key, 3)
    windows = EXPERTS // (2 * GROUP)
    first_size = jax.random.randint(key_size, (windows,), 2, CMAX + 1).astype(jnp.int32)
    forced = jax.random.randint(key_forced, (), 0, windows).astype(jnp.int32)
    first_size = jnp.where(jnp.arange(windows, dtype=jnp.int32) == forced, jnp.int32(CMAX), first_size)
    window_keys = jax.random.split(key_order, windows)
    ranks = jax.vmap(lambda one_key: jax.random.permutation(one_key, 2 * GROUP))(window_keys).astype(jnp.int32)
    labels = 2 * jnp.arange(windows, dtype=jnp.int32)[:, None] + (ranks >= first_size[:, None]).astype(jnp.int32)
    return labels.reshape(EXPERTS).astype(jnp.int32)


def set_ends(array, stream_key, least, largest):
    spot = [jax.random.randint(jax.random.fold_in(stream_key, axis), (), 0, length) for axis, length in enumerate(array.shape)]
    main_axis = array.shape.index(max(array.shape))
    next_to = spot[:main_axis] + [(spot[main_axis] + 1) % array.shape[main_axis]] + spot[main_axis + 1:]
    return array.at[tuple(spot)].set(least).at[tuple(next_to)].set(largest)


def block_levels(stream_key, shape, cuts, low, top_value):
    level, own = 1.0, jax.random.fold_in(stream_key, 6)
    for dim, shards_of in cuts:
        heights = jnp.exp(jax.random.uniform(jax.random.fold_in(own, dim), (shards_of,), jnp.float32, low / len(cuts), top_value / len(cuts)))
        level = level * jnp.repeat(heights, shape[dim] // shards_of).reshape([-1 if axis == dim else 1 for axis in range(len(shape))])
    return level


def centred(key, shape, deviation, bound, cuts=(), kind=jnp.bfloat16):
    array = deviation * jax.random.normal(key, shape, jnp.float32)
    if cuts:
        array = array * block_levels(key, shape, cuts, -0.22, 0.18)
    return jnp.clip(array, -bound, bound).astype(kind)


def setup_inputs(seed: int = 0) -> dict:
    key_of = jax.random.split(jax.random.key(seed), 6)
    expert_rows = draw_expert_rows(jax.random.fold_in(key_of[5], 71), 0)
    sketch = centred(key_of[1], (D, RANK), D ** -0.5, 0.078125, ((0, 2),))
    permutation = jax.vmap(lambda own: jax.random.permutation(own, FF))(jax.random.split(key_of[2], EXPERTS)).reshape((EXPERTS, FF)).astype(jnp.int32)
    clusters = draw_clusters(jax.random.fold_in(key_of[5], 71), 0)
    frequency = set_ends(jax.random.randint(key_of[4], (EXPERTS,), 20, 65), jax.random.fold_in(key_of[4], 1), 20, 64).astype(jnp.int32)
    return {"expert_rows": expert_rows, "sketch": sketch, "permutation": permutation, "clusters": clusters, "frequency": frequency}


def cluster_tables(clusters, frequency):
    expert_count = clusters.shape[0]
    cluster_count = expert_count // GROUP
    membership = clusters[None, :] == jnp.arange(cluster_count, dtype=jnp.int32)[:, None]
    freq_real = frequency.astype(jnp.float32)
    cluster_totals = lax.optimization_barrier(jnp.sum(jnp.where(membership, freq_real[None, :], jnp.float32(0.0)), axis=1))
    own_total = lax.optimization_barrier(jnp.sum(jnp.where(membership, cluster_totals[:, None], jnp.float32(0.0)), axis=0))
    merge_weight = (freq_real / own_total).astype(jnp.bfloat16)
    cluster_sizes = lax.optimization_barrier(jnp.sum(membership.astype(jnp.int32), axis=1))
    first_slot = jnp.cumsum(cluster_sizes) - cluster_sizes
    sorted_experts = jnp.argsort(clusters, stable=True).astype(jnp.int32)
    slot_range = jnp.arange(CMAX, dtype=jnp.int32)
    slot_live = slot_range[None, :] < cluster_sizes[:, None]
    slot_index = jnp.clip(first_slot[:, None] + slot_range[None, :], 0, expert_count - 1).astype(jnp.int32)
    members = sorted_experts[slot_index]
    return (merge_weight, members, slot_live)

def reference(expert_rows, sketch, permutation, clusters, frequency):
    expert_count = clusters.shape[0]
    cluster_count = expert_count // GROUP
    merge_weight, members, slot_live = cluster_tables(clusters, frequency)
    inverse = jnp.argsort(permutation, axis=1).astype(jnp.int32)
    inv_root = 1.0 / math.sqrt(FF)

    def cluster_work(cluster_id):
        chosen = members[cluster_id]
        slot_alive = slot_live[cluster_id]
        picked = expert_rows[chosen]
        moved = jnp.take_along_axis(picked, inverse[chosen][:, :, None], axis=1)
        merge_scale = jnp.where(slot_alive, merge_weight[chosen], jnp.zeros((), jnp.bfloat16))
        full = jnp.einsum('m,mfd->fd', merge_scale.astype(jnp.float32), moved.astype(jnp.float32), precision=lax.Precision.HIGHEST).astype(jnp.bfloat16)
        sketched = jnp.dot(full.astype(jnp.float32), sketch.astype(jnp.float32), preferred_element_type=jnp.float32)
        gram_matrix = jnp.dot(sketched.T, sketched, precision=lax.Precision.HIGHEST) / FF
        cholesky_factor = jnp.linalg.cholesky(gram_matrix)
        orth = jax.scipy.linalg.solve_triangular(cholesky_factor, sketched.T, lower=True).T
        coef = jnp.dot(orth.astype(jnp.bfloat16).T.astype(jnp.float32), full.astype(jnp.float32), preferred_element_type=jnp.float32) * inv_root
        return (full, orth, coef)
    full_all, orth_all, coef_all = lax.map(cluster_work, jnp.arange(cluster_count, dtype=jnp.int32))
    shard_count = N_SHARD
    block_cols = D // (shard_count * GROUP)
    merged = full_all.reshape(cluster_count, FF, shard_count, GROUP, block_cols)
    merged = merged.transpose(0, 3, 1, 2, 4).reshape(expert_count, FF, shard_count * block_cols)
    coefficients = coef_all.reshape(cluster_count, RANK, shard_count, GROUP, block_cols)
    coefficients = coefficients.transpose(0, 3, 1, 2, 4).reshape(expert_count, RANK, shard_count * block_cols)
    basis = orth_all.reshape(expert_count, FF // GROUP, RANK)
    return (merged, basis, coefficients)
```

```python
import math

import jax
import jax.numpy as jnp
from jax import lax
from jax.experimental import pallas as pl
from jax.experimental.pallas import tpu as pltpu
from jax.sharding import PartitionSpec as P

GROUP = 4
MESH = pl.DeviceIdType.MESH
LIMIT = 60 * 1024 * 1024


def column_chunks(width):
    chunks, start = [], 0
    while start < width:
        step = min(256, width - start)
        chunks.append((start, step))
        start += step
    return chunks


def merge_kernel(
    mix_ref,
    perm_ref,
    rows_ref,
    sketch_ref,
    merged_ref,
    full_ref,
    peer_perm,
    onehot,
    blocks,
    kept,
    zsend,
    zrecv,
    sk,
    part,
    core_rx,
    summed,
    group_rx,
    mine,
    gathered,
    perm_send,
    perm_recv,
    own_sem,
    sk_sem,
    row_send,
    row_recv,
    z_send,
    z_recv,
    core_send,
    core_recv,
    rs_send,
    rs_recv,
    ag_send,
    ag_recv,
    fw_send,
    fw_recv,
):
    position = lax.axis_index("expert")
    core = lax.axis_index("shard")
    slot = lax.rem(position, GROUP)
    plane = position - slot
    other_core = 1 - core
    ff, width = merged_ref.shape
    tile = ff // GROUP
    half = tile // 2
    rank = full_ref.shape[1]
    chunks = column_chunks(width)
    peer_slot = {
        0: slot,
        1: slot + 1 - 2 * lax.rem(slot, 2),
        2: slot + 2 - 4 * lax.div(slot, 2),
        3: 3 - slot,
    }
    peer = {d: {"expert": plane + peer_slot[d]} for d in (1, 2, 3)}
    across = {"expert": position + 4 - 8 * lax.rem(lax.div(position, 4), 2)}
    beside = {"shard": other_core}

    barrier = pltpu.get_barrier_semaphore()
    for target in (peer[1], peer[2], peer[3], across, beside):
        pl.semaphore_signal(barrier, inc=1, device_id=target, device_id_type=MESH)

    own_copy = pltpu.make_async_copy(
        rows_ref.at[:, pl.ds(pl.multiple_of(slot * width, 128), width)], blocks.at[0], own_sem
    )
    own_copy.start()
    sk_copy = pltpu.make_async_copy(
        sketch_ref.at[pl.ds(pl.multiple_of(slot * width, 128), width), :], sk, sk_sem
    )
    sk_copy.start()
    pl.semaphore_wait(barrier, 5)

    def remote(src, dst, send, recv, target):
        return pltpu.make_async_remote_copy(
            src_ref=src,
            dst_ref=dst,
            send_sem=send,
            recv_sem=recv,
            device_id=target,
            device_id_type=MESH,
        )

    perm_copies = {
        d: remote(perm_ref, peer_perm.at[d - 1], perm_send.at[d - 1], perm_recv.at[d - 1], peer[d])
        for d in (3, 1, 2)
    }
    for copy in perm_copies.values():
        copy.start()
    row_copies = {}
    for c, (start, step) in enumerate(chunks):
        for d in (3, 1, 2):
            first = pl.multiple_of(peer_slot[d] * width + start, 128)
            row_copies[c, d] = remote(
                rows_ref.at[:, pl.ds(first, step)],
                blocks.at[d, :, pl.ds(start, step)],
                row_send.at[c, d - 1],
                row_recv.at[c, d - 1],
                peer[d],
            )
            row_copies[c, d].start()

    def build(d, values):
        @pl.loop(0, 2 * GROUP)
        def _(t):
            first = pl.multiple_of(t * half, half)
            index = lax.broadcasted_iota(jnp.int32, (half, ff), 0) + first
            onehot[d, pl.ds(first, half), :] = jnp.where(index == values, 1.0, 0.0).astype(
                jnp.bfloat16
            )

    build(0, perm_ref[...])
    for d in (1, 2, 3):
        perm_copies[d].wait()
        build(d, peer_perm[d - 1])
    own_copy.wait()
    sk_copy.wait()

    def z_copy(c, t):
        start, step = chunks[c]
        first = pl.multiple_of(t * tile, tile)
        view = (pl.ds(first, tile), pl.ds(start, step))
        return remote(zsend.at[view], zrecv.at[view], z_send.at[c, t], z_recv.at[c, t], across)

    def compute(c):
        start, step = chunks[c]
        for d in (1, 2, 3):
            row_copies[c, d].wait()

        @pl.loop(0, GROUP)
        def _(t):
            first = pl.multiple_of(t * tile, tile)
            keep = jnp.zeros((tile, step), jnp.float32)
            give = jnp.zeros((tile, step), jnp.float32)
            for d in range(4):
                moved = jnp.dot(
                    onehot[d, pl.ds(first, tile), :],
                    blocks[d, :, start : start + step],
                    preferred_element_type=jnp.float32,
                )
                keep = keep + mix_ref[0, d] * moved
                give = give + mix_ref[1, d] * moved
            kept[pl.ds(first, tile), start : start + step] = keep
            zsend[pl.ds(first, tile), start : start + step] = give.astype(jnp.bfloat16)
            z_copy(c, t).start()

    def finalize(c, t):
        start, step = chunks[c]
        first = pl.multiple_of(t * tile, tile)
        z_copy(c, t).wait()
        merged_ref[pl.ds(first, tile), start : start + step] = (
            kept[pl.ds(first, tile), start : start + step]
            + zrecv[pl.ds(first, tile), start : start + step].astype(jnp.float32)
        ).astype(jnp.bfloat16)

    last = len(chunks) - 1
    for c in range(last + 1):
        compute(c)
        if c >= 1:

            @pl.loop(0, GROUP)
            def _(t):
                finalize(c - 1, t)

    def core_copy(t):
        first = pl.multiple_of(t * tile + other_core * half, half)
        return remote(
            part.at[pl.ds(first, half), :],
            core_rx.at[t],
            core_send.at[t],
            core_recv.at[t],
            beside,
        )

    @pl.loop(0, GROUP)
    def _(t):
        finalize(last, t)
        first = pl.multiple_of(t * tile, tile)
        part[pl.ds(first, tile), :] = jnp.dot(
            merged_ref[pl.ds(first, tile), :], sk[...], preferred_element_type=jnp.float32
        )
        core_copy(t).start()

    @pl.loop(0, GROUP)
    def _(t):
        core_copy(t).wait()
        first = pl.multiple_of(t * tile + core * half, half)
        summed[t] = part[pl.ds(first, half), :] + core_rx[t]

    rs_copies = {}
    for d in (3, 1, 2):
        rs_copies[d] = remote(
            summed.at[peer_slot[d]],
            group_rx.at[d - 1],
            rs_send.at[d - 1],
            rs_recv.at[d - 1],
            peer[d],
        )
        rs_copies[d].start()
    total = summed[slot]
    for d in (1, 2, 3):
        rs_copies[d].wait()
        total = total + group_rx[d - 1]
    mine[...] = total
    place = slot * 2 + core
    ag_copies = {}
    for d in (3, 1, 2):
        ag_copies[d] = remote(
            mine, gathered.at[place], ag_send.at[d - 1], ag_recv.at[d - 1], peer[d]
        )
        ag_copies[d].start()
    forwards = [remote(mine, gathered.at[place], fw_send.at[0], fw_recv.at[0], beside)]
    forwards[0].start()
    gathered[place] = total
    for d in (1, 2, 3):
        ag_copies[d].wait()
        came = peer_slot[d] * 2 + core
        forwards.append(
            remote(gathered.at[came], gathered.at[came], fw_send.at[d], fw_recv.at[d], beside)
        )
        forwards[d].start()
    for copy in forwards:
        copy.wait()
    for b in range(2 * GROUP):
        full_ref[b * half : (b + 1) * half, :] = gathered[b]


def merge(mix, perm, rows, sketch):
    ff, part_cols = rows.shape
    width = part_cols // GROUP
    rank = sketch.shape[1]
    half = ff // (2 * GROUP)
    chunks = len(column_chunks(width))
    dma = pltpu.SemaphoreType.DMA
    vmem = pl.BlockSpec(memory_space=pltpu.VMEM)
    f32, bf16 = jnp.float32, jnp.bfloat16
    return pl.pallas_call(
        merge_kernel,
        out_shape=(
            jax.ShapeDtypeStruct((ff, width), bf16),
            jax.ShapeDtypeStruct((ff, rank), f32),
        ),
        in_specs=[
            pl.BlockSpec(memory_space=pltpu.SMEM),
            vmem,
            pl.BlockSpec(memory_space=pl.ANY),
            pl.BlockSpec(memory_space=pl.ANY),
        ],
        out_specs=(vmem, vmem),
        scratch_shapes=[
            pltpu.VMEM((3, 1, ff), jnp.int32),
            pltpu.VMEM((4, ff, ff), bf16),
            pltpu.VMEM((4, ff, width), bf16),
            pltpu.VMEM((ff, width), f32),
            pltpu.VMEM((ff, width), bf16),
            pltpu.VMEM((ff, width), bf16),
            pltpu.VMEM((width, rank), bf16),
            pltpu.VMEM((ff, rank), f32),
            pltpu.VMEM((GROUP, half, rank), f32),
            pltpu.VMEM((GROUP, half, rank), f32),
            pltpu.VMEM((3, half, rank), f32),
            pltpu.VMEM((half, rank), f32),
            pltpu.VMEM((2 * GROUP, half, rank), f32),
            dma((3,)),
            dma((3,)),
            dma,
            dma,
            dma((chunks, 3)),
            dma((chunks, 3)),
            dma((chunks, GROUP)),
            dma((chunks, GROUP)),
            dma((GROUP,)),
            dma((GROUP,)),
            dma((3,)),
            dma((3,)),
            dma((3,)),
            dma((3,)),
            dma((4,)),
            dma((4,)),
        ],
        compiler_params=pltpu.CompilerParams(
            collective_id=0, has_side_effects=True, vmem_limit_bytes=LIMIT
        ),
        name="merge",
    )(mix, perm, rows, sketch)


def exact_dot(left, right, dims):
    return lax.dot_general(
        left,
        right,
        (dims, ((), ())),
        precision=lax.Precision.HIGHEST,
        preferred_element_type=jnp.float32,
    )


def inverse_factor(matrix):
    size = matrix.shape[0]
    groups = [matrix[g * 8 : g * 8 + 8, :] for g in range(size // 8)]
    lane = lax.broadcasted_iota(jnp.int32, (8, size), 1)
    line = lax.broadcasted_iota(jnp.int32, (8, size), 0)
    for j in range(size):
        g, r = j // 8, j % 8
        row = groups[g][r : r + 1, :]
        inverse = 1.0 / jnp.broadcast_to(row[:, j : j + 1], (8, size))
        here = lane == j
        scaled = jnp.where(here, inverse, jnp.broadcast_to(row, (8, size)) * inverse)
        for h in range(g, size // 8):
            column = jnp.broadcast_to(groups[h][:, j : j + 1], (8, size))
            new = jnp.where(here, 0.0, groups[h]) - column * scaled
            groups[h] = jnp.where(line > r, new, groups[h]) if h == g else new
    out = []
    for h in range(size // 8):
        diagonal = lane == line + h * 8
        pivot = jnp.sum(jnp.where(diagonal, groups[h], 0.0), axis=1, keepdims=True)
        root = 1.0 / jnp.sqrt(pivot)
        body = jnp.where(lane < line + h * 8, groups[h], jnp.where(diagonal, 1.0, 0.0))
        out.append(body * root)
    return jnp.concatenate(out, axis=0)


def factor_kernel(full_ref, merged_ref, basis_ref, coef_ref):
    ff, rank = full_ref.shape
    half = rank // 2
    sketched = full_ref[...]
    turned = sketched.T
    gram = exact_dot(turned, sketched, ((1,), (0,))) / ff
    first = inverse_factor(gram[:half, :half])
    lower = exact_dot(gram[half:, :half], first, ((1,), (1,)))
    second = inverse_factor(gram[half:, half:] - exact_dot(lower, lower, ((1,), (1,))))
    corner = -exact_dot(second, exact_dot(lower, first, ((1,), (0,))), ((1,), (0,)))
    inverse = jnp.concatenate(
        [
            jnp.concatenate([first, jnp.zeros((half, half), jnp.float32)], axis=1),
            jnp.concatenate([corner, second], axis=1),
        ],
        axis=0,
    )
    turned_orth = exact_dot(inverse, turned, ((1,), (0,))).astype(jnp.bfloat16)
    coef_ref[...] = jnp.dot(
        turned_orth, merged_ref[...], preferred_element_type=jnp.float32
    ) * (1.0 / math.sqrt(ff))
    count = basis_ref.shape[0]
    place = lax.rem(lax.axis_index("expert"), GROUP) * 2 + lax.axis_index("shard")
    mine = full_ref[pl.ds(pl.multiple_of(place * count, count), count), :]
    basis_ref[...] = exact_dot(mine, inverse, ((1,), (1,)))


def factor(full, merged):
    ff, rank = full.shape
    vmem = pl.BlockSpec(memory_space=pltpu.VMEM)
    return pl.pallas_call(
        factor_kernel,
        out_shape=(
            jax.ShapeDtypeStruct((ff // (2 * GROUP), rank), jnp.float32),
            jax.ShapeDtypeStruct((rank, merged.shape[1]), jnp.float32),
        ),
        in_specs=[vmem, vmem],
        out_specs=(vmem, vmem),
        compiler_params=pltpu.CompilerParams(vmem_limit_bytes=LIMIT),
        name="factor",
    )(full, merged)


def mixing_pairs(clusters, frequency):
    count = clusters.shape[0]
    position = lax.axis_index("expert")
    own = position // GROUP
    freq = frequency.astype(jnp.float32)
    same = clusters[:, None] == clusters[None, :]
    totals = jnp.sum(jnp.where(same, freq[None, :], 0.0), axis=1)
    weight = (freq / totals).astype(jnp.bfloat16).astype(jnp.float32)
    sources = own * GROUP + ((position % GROUP) ^ jnp.arange(GROUP, dtype=jnp.int32))
    chosen = sources[:, None] == jnp.arange(count, dtype=jnp.int32)[None, :]
    wanted = jnp.stack([own, own ^ 1])
    picked = chosen[None, :, :] & (clusters[None, None, :] == wanted[:, None, None])
    return jnp.sum(jnp.where(picked, weight[None, None, :], 0.0), axis=2)


def on_device(expert_rows, sketch, permutation, clusters, frequency):
    mix = mixing_pairs(clusters, frequency)
    merged, full = merge(mix, permutation, expert_rows[0], sketch)
    basis, coef = factor(full, merged)
    return merged[None], basis[None], coef[None]


def solution(mesh):
    return jax.shard_map(
        on_device,
        mesh=mesh,
        in_specs=(P("expert", None, "shard"), P("shard", None), P("expert", None), P(), P()),
        out_specs=(
            P("expert", None, "shard"),
            P("expert", "shard", None),
            P("expert", None, "shard"),
        ),
        check_vma=False,
    )
```

```python
import math

import jax
import jax.numpy as jnp
from jax import lax
from jax.experimental import pallas as pl
from jax.experimental.pallas import tpu as pltpu
from jax.sharding import PartitionSpec as P

GROUP = 4
MESH = pl.DeviceIdType.MESH
LIMIT = 60 * 1024 * 1024


def column_chunks(width):
    chunks, start = [], 0
    while start < width:
        step = min(256, width - start)
        chunks.append((start, step))
        start += step
    return chunks


def merge_kernel(
    clusters_ref,
    frequency_ref,
    perm_ref,
    rows_ref,
    sketch_ref,
    merged_ref,
    full_ref,
    peer_perm,
    onehot,
    blocks,
    kept,
    wide_send,
    wide_recv,
    zsend,
    zrecv,
    sk,
    part,
    core_rx,
    summed,
    group_rx,
    mine,
    gathered,
    perm_send,
    perm_recv,
    own_sem,
    sk_sem,
    row_send,
    row_recv,
    z_send,
    z_recv,
    core_send,
    core_recv,
    rs_send,
    rs_recv,
    ag_send,
    ag_recv,
    fw_send,
    fw_recv,
):
    position = lax.axis_index("expert")
    core = lax.axis_index("shard")
    slot = lax.rem(position, GROUP)
    plane = position - slot
    other_core = 1 - core
    ff, width = merged_ref.shape
    tile = ff // GROUP
    half = tile // 2
    chunks = column_chunks(width)
    lanes = chunks[0][1]
    peer_slot = {
        0: slot,
        1: slot + 1 - 2 * lax.rem(slot, 2),
        2: slot + 2 - 4 * lax.div(slot, 2),
        3: 3 - slot,
    }
    peer = {d: {"expert": plane + peer_slot[d]} for d in (1, 2, 3)}
    across = {"expert": position + 4 - 8 * lax.rem(lax.div(position, 4), 2)}
    beside = {"shard": other_core}

    barrier = pltpu.get_barrier_semaphore()
    for target in (peer[1], peer[2], peer[3], across, beside):
        pl.semaphore_signal(barrier, inc=1, device_id=target, device_id_type=MESH)

    own_copy = pltpu.make_async_copy(
        rows_ref.at[:, pl.ds(pl.multiple_of(slot * width, 128), width)], blocks.at[0], own_sem
    )
    own_copy.start()
    sk_copy = pltpu.make_async_copy(
        sketch_ref.at[pl.ds(pl.multiple_of(slot * width, 128), width), :], sk, sk_sem
    )
    sk_copy.start()
    pl.semaphore_wait(barrier, 5)

    def remote(src, dst, send, recv, target):
        return pltpu.make_async_remote_copy(
            src_ref=src,
            dst_ref=dst,
            send_sem=send,
            recv_sem=recv,
            device_id=target,
            device_id_type=MESH,
        )

    perm_copies = {
        d: remote(perm_ref, peer_perm.at[d - 1], perm_send.at[d - 1], perm_recv.at[d - 1], peer[d])
        for d in (3, 1, 2)
    }
    for copy in perm_copies.values():
        copy.start()
    row_copies = {}
    for c, (start, step) in enumerate(chunks):
        for d in (3, 1, 2):
            first = pl.multiple_of(peer_slot[d] * width + start, 128)
            row_copies[c, d] = remote(
                rows_ref.at[:, pl.ds(first, step)],
                blocks.at[d, :, pl.ds(start, step)],
                row_send.at[c, d - 1],
                row_recv.at[c, d - 1],
                peer[d],
            )
            row_copies[c, d].start()

    def build(d, values):
        @pl.loop(0, 2 * GROUP)
        def _(t):
            first = pl.multiple_of(t * half, half)
            index = lax.broadcasted_iota(jnp.int32, (half, ff), 0) + first
            onehot[d, pl.ds(first, half), :] = jnp.where(index == values, 1.0, 0.0).astype(
                jnp.bfloat16
            )

    build(0, perm_ref[...])
    for d in (1, 2, 3):
        perm_copies[d].wait()
        build(d, peer_perm[d - 1])
    window = position - lax.rem(position, 2 * GROUP)
    own = lax.div(position, GROUP)
    other = own + 1 - 2 * lax.rem(own, 2)

    def shares(cluster):
        total = jnp.int32(0)
        for e in range(2 * GROUP):
            member = clusters_ref[window + e] == cluster
            total = total + jnp.where(member, frequency_ref[window + e], 0)
        total = jnp.full((1, lanes), total).astype(jnp.float32)
        rows = []
        for d in range(GROUP):
            e = plane + peer_slot[d]
            part_of = jnp.where(clusters_ref[e] == cluster, frequency_ref[e], 0)
            weight = jnp.full((1, lanes), part_of).astype(jnp.float32) / total
            rows.append(weight.astype(jnp.bfloat16).astype(jnp.float32))
        return rows

    keep_share, give_share = shares(own), shares(other)
    own_copy.wait()
    sk_copy.wait()

    def tile_of(i):
        low = lax.rem(slot + 3 - i, 2)
        high = lax.rem(lax.div(slot, 2) + lax.div(3 - i, 2), 2)
        return high * 2 + low

    def z_copy(c, t):
        start, step = chunks[c]
        rows = pl.ds(pl.multiple_of(t * tile, tile), tile)
        if c == 0:
            source, target = wide_send.at[rows, :], wide_recv.at[rows, :]
        else:
            view = (rows, pl.ds(start - lanes, step))
            source, target = zsend.at[view], zrecv.at[view]
        return remote(source, target, z_send.at[c, t], z_recv.at[c, t], across)

    def compute(c):
        start, step = chunks[c]
        for d in (1, 2, 3):
            row_copies[c, d].wait()

        @pl.loop(0, GROUP)
        def _(i):
            t = tile_of(i)
            rows = pl.ds(pl.multiple_of(t * tile, tile), tile)
            keep = jnp.zeros((tile, step), jnp.float32)
            give = jnp.zeros((tile, step), jnp.float32)
            for d in range(GROUP):
                moved = jnp.dot(
                    onehot[d, rows, :],
                    blocks[d, :, start : start + step],
                    preferred_element_type=jnp.float32,
                )
                keep = keep + keep_share[d][:, :step] * moved
                give = give + give_share[d][:, :step] * moved
            kept[rows, start : start + step] = keep
            if c == 0:
                wide_send[rows, :] = give
            else:
                zsend[rows, start - lanes : start - lanes + step] = give.astype(jnp.bfloat16)
            z_copy(c, t).start()

    def finalize(c, t):
        start, step = chunks[c]
        rows = pl.ds(pl.multiple_of(t * tile, tile), tile)
        z_copy(c, t).wait()
        if c == 0:
            came = wide_recv[rows, :]
        else:
            came = zrecv[rows, start - lanes : start - lanes + step].astype(jnp.float32)
        merged_ref[rows, start : start + step] = (
            kept[rows, start : start + step] + came
        ).astype(jnp.bfloat16)

    last = len(chunks) - 1
    for c in range(last + 1):
        compute(c)
        if c >= 1:

            @pl.loop(0, GROUP)
            def _(i):
                finalize(c - 1, tile_of(i))

    def core_copy(t):
        first = pl.multiple_of(t * tile + other_core * half, half)
        return remote(
            part.at[pl.ds(first, half), :],
            core_rx.at[t],
            core_send.at[t],
            core_recv.at[t],
            beside,
        )

    rs_copies = {}

    def gather_tile(d):
        t = peer_slot[d]
        core_copy(t).wait()
        first = pl.multiple_of(t * tile + core * half, half)
        summed[t] = part[pl.ds(first, half), :] + core_rx[t]
        if d:
            rs_copies[d] = remote(
                summed.at[t], group_rx.at[d - 1], rs_send.at[d - 1], rs_recv.at[d - 1], peer[d]
            )
            rs_copies[d].start()

    for d in (3, 2, 1, 0):
        t = peer_slot[d]
        finalize(last, t)
        rows = pl.ds(pl.multiple_of(t * tile, tile), tile)
        part[rows, :] = jnp.dot(merged_ref[rows, :], sk[...], preferred_element_type=jnp.float32)
        core_copy(t).start()
        if d < 3:
            gather_tile(d + 1)
    gather_tile(0)
    total = summed[slot]
    for d in (3, 2, 1):
        rs_copies[d].wait()
        total = total + group_rx[d - 1]
    mine[...] = total
    place = slot * 2 + core
    ag_copies = {}
    for d in (3, 1, 2):
        ag_copies[d] = remote(
            mine, gathered.at[place], ag_send.at[d - 1], ag_recv.at[d - 1], peer[d]
        )
        ag_copies[d].start()
    forwards = [remote(mine, gathered.at[place], fw_send.at[0], fw_recv.at[0], beside)]
    forwards[0].start()
    gathered[place] = total
    for d in (1, 2, 3):
        ag_copies[d].wait()
        came = peer_slot[d] * 2 + core
        forwards.append(
            remote(gathered.at[came], gathered.at[came], fw_send.at[d], fw_recv.at[d], beside)
        )
        forwards[d].start()
    for copy in forwards:
        copy.wait()
    for b in range(2 * GROUP):
        full_ref[b * half : (b + 1) * half, :] = gathered[b]


def merge(clusters, frequency, perm, rows, sketch):
    ff, part_cols = rows.shape
    width = part_cols // GROUP
    rank = sketch.shape[1]
    half = ff // (2 * GROUP)
    lanes = column_chunks(width)[0][1]
    chunks = len(column_chunks(width))
    dma = pltpu.SemaphoreType.DMA
    vmem = pl.BlockSpec(memory_space=pltpu.VMEM)
    f32, bf16 = jnp.float32, jnp.bfloat16
    return pl.pallas_call(
        merge_kernel,
        out_shape=(
            jax.ShapeDtypeStruct((ff, width), bf16),
            jax.ShapeDtypeStruct((ff, rank), f32),
        ),
        in_specs=[
            pl.BlockSpec(memory_space=pltpu.SMEM),
            pl.BlockSpec(memory_space=pltpu.SMEM),
            vmem,
            pl.BlockSpec(memory_space=pl.ANY),
            pl.BlockSpec(memory_space=pl.ANY),
        ],
        out_specs=(vmem, vmem),
        scratch_shapes=[
            pltpu.VMEM((3, 1, ff), jnp.int32),
            pltpu.VMEM((4, ff, ff), bf16),
            pltpu.VMEM((4, ff, width), bf16),
            pltpu.VMEM((ff, width), f32),
            pltpu.VMEM((ff, lanes), f32),
            pltpu.VMEM((ff, lanes), f32),
            pltpu.VMEM((ff, width - lanes), bf16),
            pltpu.VMEM((ff, width - lanes), bf16),
            pltpu.VMEM((width, rank), bf16),
            pltpu.VMEM((ff, rank), f32),
            pltpu.VMEM((GROUP, half, rank), f32),
            pltpu.VMEM((GROUP, half, rank), f32),
            pltpu.VMEM((3, half, rank), f32),
            pltpu.VMEM((half, rank), f32),
            pltpu.VMEM((2 * GROUP, half, rank), f32),
            dma((3,)),
            dma((3,)),
            dma,
            dma,
            dma((chunks, 3)),
            dma((chunks, 3)),
            dma((chunks, GROUP)),
            dma((chunks, GROUP)),
            dma((GROUP,)),
            dma((GROUP,)),
            dma((3,)),
            dma((3,)),
            dma((3,)),
            dma((3,)),
            dma((4,)),
            dma((4,)),
        ],
        compiler_params=pltpu.CompilerParams(
            collective_id=0, has_side_effects=True, vmem_limit_bytes=LIMIT
        ),
        name="merge",
    )(clusters, frequency, perm, rows, sketch)


def exact_dot(left, right, dims):
    return lax.dot_general(
        left,
        right,
        (dims, ((), ())),
        precision=lax.Precision.HIGHEST,
        preferred_element_type=jnp.float32,
    )


def spread(value, row, column):
    size = value.shape[1]
    line = jnp.broadcast_to(value[row : row + 1, :], (8, size))
    return jnp.broadcast_to(line[:, column : column + 1], (8, size))


def inverse_factor(matrix):
    size = matrix.shape[0]
    count = size // 8
    groups = [matrix[g * 8 : g * 8 + 8, :] for g in range(count)]
    lane = lax.broadcasted_iota(jnp.int32, (8, size), 1)
    line = lax.broadcasted_iota(jnp.int32, (8, size), 0)
    out = []
    for g in range(count):
        base = g * 8
        inside = (lane >= base) & (lane < base + 8)
        pivot = [[spread(groups[g], r, base + s) for s in range(r + 1)] for r in range(8)]
        seeded = jnp.where(inside, jnp.where(lane == line + base, 1.0, 0.0), groups[g])
        rows = [jnp.broadcast_to(seeded[r : r + 1, :], (8, size)) for r in range(8)]
        inverses, factors = [], {}
        for s in range(8):
            inverse = 1.0 / pivot[s][s]
            inverses.append(inverse)
            for r in range(s + 1, 8):
                factors[r, s] = pivot[r][s] * inverse
            for r in range(s + 1, 8):
                for t in range(s + 1, r + 1):
                    pivot[r][t] = pivot[r][t] - factors[r, s] * pivot[t][s]
                rows[r] = rows[r] - factors[r, s] * rows[s]
        block = rows[7] * lax.rsqrt(pivot[7][7])
        for r in range(7):
            block = jnp.where(line == r, rows[r] * lax.rsqrt(pivot[r][r]), block)
        out.append(jnp.where(lane <= line + base, block, 0.0))
        if g == count - 1:
            break
        back = [None] * 8
        for s in reversed(range(8)):
            value = rows[s] * inverses[s]
            for r in reversed(range(s + 1, 8)):
                value = value - factors[r, s] * back[r]
            back[s] = value
        for h in range(g + 1, count):
            columns = [
                jnp.broadcast_to(groups[h][:, base + s : base + s + 1], (8, size))
                for s in range(8)
            ]
            value = jnp.where(inside, 0.0, groups[h])
            terms = [columns[s] * back[s] for s in range(8)]
            groups[h] = value - (
                ((terms[0] + terms[1]) + (terms[2] + terms[3]))
                + ((terms[4] + terms[5]) + (terms[6] + terms[7]))
            )
    return jnp.concatenate(out, axis=0)


def factor_kernel(full_ref, merged_ref, out_ref, basis_ref, coef_ref, out_sem):
    out_copy = pltpu.make_async_copy(merged_ref, out_ref, out_sem)
    out_copy.start()
    ff, rank = full_ref.shape
    half = rank // 2
    sketched = full_ref[...]
    turned = sketched.T
    gram = exact_dot(turned, sketched, ((1,), (0,))) / ff
    first = inverse_factor(gram[:half, :half])
    lower = exact_dot(gram[half:, :half], first, ((1,), (1,)))
    second = inverse_factor(gram[half:, half:] - exact_dot(lower, lower, ((1,), (1,))))
    corner = -exact_dot(second, exact_dot(lower, first, ((1,), (0,))), ((1,), (0,)))
    inverse = jnp.concatenate(
        [
            jnp.concatenate([first, jnp.zeros((half, half), jnp.float32)], axis=1),
            jnp.concatenate([corner, second], axis=1),
        ],
        axis=0,
    )
    turned_orth = exact_dot(inverse, turned, ((1,), (0,))).astype(jnp.bfloat16)
    coef_ref[...] = jnp.dot(
        turned_orth, merged_ref[...], preferred_element_type=jnp.float32
    ) * (1.0 / math.sqrt(ff))
    count = basis_ref.shape[0]
    place = lax.rem(lax.axis_index("expert"), GROUP) * 2 + lax.axis_index("shard")
    mine = full_ref[pl.ds(pl.multiple_of(place * count, count), count), :]
    basis_ref[...] = exact_dot(mine, inverse, ((1,), (1,)))
    out_copy.wait()


def factor(full, merged):
    ff, rank = full.shape
    vmem = pl.BlockSpec(memory_space=pltpu.VMEM)
    return pl.pallas_call(
        factor_kernel,
        out_shape=(
            jax.ShapeDtypeStruct(merged.shape, merged.dtype),
            jax.ShapeDtypeStruct((ff // (2 * GROUP), rank), jnp.float32),
            jax.ShapeDtypeStruct((rank, merged.shape[1]), jnp.float32),
        ),
        in_specs=[vmem, vmem],
        out_specs=(pl.BlockSpec(memory_space=pl.ANY), vmem, vmem),
        scratch_shapes=[pltpu.SemaphoreType.DMA],
        compiler_params=pltpu.CompilerParams(vmem_limit_bytes=LIMIT),
        name="factor",
    )(full, merged)


def on_device(expert_rows, sketch, permutation, clusters, frequency):
    merged, full = merge(clusters, frequency, permutation, expert_rows[0], sketch)
    merged, basis, coef = factor(full, merged)
    return merged[None], basis[None], coef[None]


def solution(mesh):
    return jax.shard_map(
        on_device,
        mesh=mesh,
        in_specs=(P("expert", None, "shard"), P("shard", None), P("expert", None), P(), P()),
        out_specs=(
            P("expert", None, "shard"),
            P("expert", "shard", None),
            P("expert", None, "shard"),
        ),
        check_vma=False,
    )
```

```python
import math

import jax
import jax.numpy as jnp
from jax import lax
from jax.experimental import pallas as pl
from jax.experimental.pallas import tpu as pltpu
from jax.sharding import PartitionSpec as P

GROUP = 4
MESH = pl.DeviceIdType.MESH
LIMIT = 60 * 1024 * 1024


def column_chunks(width):
    chunks, start = [], 0
    while start < width:
        step = min(256, width - start)
        chunks.append((start, step))
        start += step
    return chunks


def merge_kernel(
    clusters_ref,
    frequency_ref,
    perm_ref,
    rows_ref,
    sketch_ref,
    merged_ref,
    full_ref,
    total_ref,
    peer_perm,
    onehot,
    blocks,
    kept,
    wide_send,
    wide_recv,
    zsend,
    zrecv,
    sk,
    part,
    core_rx,
    summed,
    group_rx,
    mine,
    gathered,
    perm_send,
    perm_recv,
    own_sem,
    sk_sem,
    row_send,
    row_recv,
    z_send,
    z_recv,
    core_send,
    core_recv,
    rs_send,
    rs_recv,
    ag_send,
    ag_recv,
    fw_send,
    fw_recv,
):
    position = lax.axis_index("expert")
    core = lax.axis_index("shard")
    slot = lax.rem(position, GROUP)
    plane = position - slot
    other_core = 1 - core
    ff, width = merged_ref.shape
    tile = ff // GROUP
    half = tile // 2
    chunks = column_chunks(width)
    lanes = chunks[0][1]
    peer_slot = {
        0: slot,
        1: slot + 1 - 2 * lax.rem(slot, 2),
        2: slot + 2 - 4 * lax.div(slot, 2),
        3: 3 - slot,
    }
    peer = {d: {"expert": plane + peer_slot[d]} for d in (1, 2, 3)}
    across = {"expert": position + 4 - 8 * lax.rem(lax.div(position, 4), 2)}
    beside = {"shard": other_core}

    barrier = pltpu.get_barrier_semaphore()
    for target in (peer[1], peer[2], peer[3], across, beside):
        pl.semaphore_signal(barrier, inc=1, device_id=target, device_id_type=MESH)

    own_copy = pltpu.make_async_copy(
        rows_ref.at[:, pl.ds(pl.multiple_of(slot * width, 128), width)], blocks.at[0], own_sem
    )
    own_copy.start()
    sk_copy = pltpu.make_async_copy(
        sketch_ref.at[pl.ds(pl.multiple_of(slot * width, 128), width), :], sk, sk_sem
    )
    sk_copy.start()
    pl.semaphore_wait(barrier, 5)

    def remote(src, dst, send, recv, target):
        return pltpu.make_async_remote_copy(
            src_ref=src,
            dst_ref=dst,
            send_sem=send,
            recv_sem=recv,
            device_id=target,
            device_id_type=MESH,
        )

    perm_copies = {
        d: remote(perm_ref, peer_perm.at[d - 1], perm_send.at[d - 1], perm_recv.at[d - 1], peer[d])
        for d in (3, 1, 2)
    }
    for copy in perm_copies.values():
        copy.start()
    row_copies = {}
    for c, (start, step) in enumerate(chunks):
        for d in (3, 1, 2):
            first = pl.multiple_of(peer_slot[d] * width + start, 128)
            row_copies[c, d] = remote(
                rows_ref.at[:, pl.ds(first, step)],
                blocks.at[d, :, pl.ds(start, step)],
                row_send.at[c, d - 1],
                row_recv.at[c, d - 1],
                peer[d],
            )
            row_copies[c, d].start()

    def build(d, values):
        @pl.loop(0, 2 * GROUP)
        def _(t):
            first = pl.multiple_of(t * half, half)
            index = lax.broadcasted_iota(jnp.int32, (half, ff), 0) + first
            onehot[d, pl.ds(first, half), :] = jnp.where(index == values, 1.0, 0.0).astype(
                jnp.bfloat16
            )

    build(0, perm_ref[...])
    for d in (1, 2, 3):
        perm_copies[d].wait()
        build(d, peer_perm[d - 1])
    window = position - lax.rem(position, 2 * GROUP)
    own = lax.div(position, GROUP)
    other = own + 1 - 2 * lax.rem(own, 2)

    def shares(cluster):
        total = jnp.int32(0)
        for e in range(2 * GROUP):
            member = clusters_ref[window + e] == cluster
            total = total + jnp.where(member, frequency_ref[window + e], 0)
        total = jnp.full((1, lanes), total).astype(jnp.float32)
        rows = []
        for d in range(GROUP):
            e = plane + peer_slot[d]
            part_of = jnp.where(clusters_ref[e] == cluster, frequency_ref[e], 0)
            weight = jnp.full((1, lanes), part_of).astype(jnp.float32) / total
            rows.append(weight.astype(jnp.bfloat16).astype(jnp.float32))
        return rows

    keep_share, give_share = shares(own), shares(other)
    own_copy.wait()
    sk_copy.wait()

    def tile_of(i):
        low = lax.rem(slot + 3 - i, 2)
        high = lax.rem(lax.div(slot, 2) + lax.div(3 - i, 2), 2)
        return high * 2 + low

    def z_copy(c, t):
        start, step = chunks[c]
        rows = pl.ds(pl.multiple_of(t * tile, tile), tile)
        if c == 0:
            source, target = wide_send.at[rows, :], wide_recv.at[rows, :]
        else:
            view = (rows, pl.ds(start - lanes, step))
            source, target = zsend.at[view], zrecv.at[view]
        return remote(source, target, z_send.at[c, t], z_recv.at[c, t], across)

    def compute(c):
        start, step = chunks[c]
        for d in (1, 2, 3):
            row_copies[c, d].wait()

        @pl.loop(0, GROUP)
        def _(i):
            t = tile_of(i)
            rows = pl.ds(pl.multiple_of(t * tile, tile), tile)
            keep = jnp.zeros((tile, step), jnp.float32)
            give = jnp.zeros((tile, step), jnp.float32)
            for d in range(GROUP):
                moved = jnp.dot(
                    onehot[d, rows, :],
                    blocks[d, :, start : start + step],
                    preferred_element_type=jnp.float32,
                )
                keep = keep + keep_share[d][:, :step] * moved
                give = give + give_share[d][:, :step] * moved
            kept[rows, start : start + step] = keep
            if c == 0:
                wide_send[rows, :] = give
            else:
                zsend[rows, start - lanes : start - lanes + step] = give.astype(jnp.bfloat16)
            z_copy(c, t).start()

    def finalize(c, t):
        start, step = chunks[c]
        rows = pl.ds(pl.multiple_of(t * tile, tile), tile)
        z_copy(c, t).wait()
        if c == 0:
            came = wide_recv[rows, :]
        else:
            came = zrecv[rows, start - lanes : start - lanes + step].astype(jnp.float32)
        merged_ref[rows, start : start + step] = (
            kept[rows, start : start + step] + came
        ).astype(jnp.bfloat16)

    last = len(chunks) - 1
    for c in range(last + 1):
        compute(c)
        if c >= 1:

            @pl.loop(0, GROUP)
            def _(i):
                finalize(c - 1, tile_of(i))

    def core_copy(t):
        first = pl.multiple_of(t * tile + other_core * half, half)
        return remote(
            part.at[pl.ds(first, half), :],
            core_rx.at[t],
            core_send.at[t],
            core_recv.at[t],
            beside,
        )

    rs_copies = {}

    def gather_tile(d):
        t = peer_slot[d]
        core_copy(t).wait()
        first = pl.multiple_of(t * tile + core * half, half)
        summed[t] = part[pl.ds(first, half), :] + core_rx[t]
        if d:
            rs_copies[d] = remote(
                summed.at[t], group_rx.at[d - 1], rs_send.at[d - 1], rs_recv.at[d - 1], peer[d]
            )
            rs_copies[d].start()

    for d in (3, 2, 1, 0):
        t = peer_slot[d]
        finalize(last, t)
        rows = pl.ds(pl.multiple_of(t * tile, tile), tile)
        part[rows, :] = jnp.dot(merged_ref[rows, :], sk[...], preferred_element_type=jnp.float32)
        core_copy(t).start()
        if d < 3:
            gather_tile(d + 1)
    gather_tile(0)
    total = summed[slot]
    for d in (3, 2, 1):
        rs_copies[d].wait()
        total = total + group_rx[d - 1]
    total_ref[...] = total
    rounded = total.astype(jnp.bfloat16)
    mine[...] = rounded
    place = slot * 2 + core
    ag_copies = {}
    for d in (3, 1, 2):
        ag_copies[d] = remote(
            mine, gathered.at[place], ag_send.at[d - 1], ag_recv.at[d - 1], peer[d]
        )
        ag_copies[d].start()
    forwards = [remote(mine, gathered.at[place], fw_send.at[0], fw_recv.at[0], beside)]
    forwards[0].start()
    gathered[place] = rounded
    for d in (1, 2, 3):
        ag_copies[d].wait()
        came = peer_slot[d] * 2 + core
        forwards.append(
            remote(gathered.at[came], gathered.at[came], fw_send.at[d], fw_recv.at[d], beside)
        )
        forwards[d].start()
    for copy in forwards:
        copy.wait()
    for b in range(2 * GROUP):
        full_ref[b * half : (b + 1) * half, :] = gathered[b]


def merge(clusters, frequency, perm, rows, sketch):
    ff, part_cols = rows.shape
    width = part_cols // GROUP
    rank = sketch.shape[1]
    half = ff // (2 * GROUP)
    lanes = column_chunks(width)[0][1]
    chunks = len(column_chunks(width))
    dma = pltpu.SemaphoreType.DMA
    vmem = pl.BlockSpec(memory_space=pltpu.VMEM)
    f32, bf16 = jnp.float32, jnp.bfloat16
    return pl.pallas_call(
        merge_kernel,
        out_shape=(
            jax.ShapeDtypeStruct((ff, width), bf16),
            jax.ShapeDtypeStruct((ff, rank), bf16),
            jax.ShapeDtypeStruct((half, rank), f32),
        ),
        in_specs=[
            pl.BlockSpec(memory_space=pltpu.SMEM),
            pl.BlockSpec(memory_space=pltpu.SMEM),
            vmem,
            pl.BlockSpec(memory_space=pl.ANY),
            pl.BlockSpec(memory_space=pl.ANY),
        ],
        out_specs=(vmem, vmem, vmem),
        scratch_shapes=[
            pltpu.VMEM((3, 1, ff), jnp.int32),
            pltpu.VMEM((4, ff, ff), bf16),
            pltpu.VMEM((4, ff, width), bf16),
            pltpu.VMEM((ff, width), f32),
            pltpu.VMEM((ff, lanes), f32),
            pltpu.VMEM((ff, lanes), f32),
            pltpu.VMEM((ff, width - lanes), bf16),
            pltpu.VMEM((ff, width - lanes), bf16),
            pltpu.VMEM((width, rank), bf16),
            pltpu.VMEM((ff, rank), f32),
            pltpu.VMEM((GROUP, half, rank), f32),
            pltpu.VMEM((GROUP, half, rank), f32),
            pltpu.VMEM((3, half, rank), f32),
            pltpu.VMEM((half, rank), bf16),
            pltpu.VMEM((2 * GROUP, half, rank), bf16),
            dma((3,)),
            dma((3,)),
            dma,
            dma,
            dma((chunks, 3)),
            dma((chunks, 3)),
            dma((chunks, GROUP)),
            dma((chunks, GROUP)),
            dma((GROUP,)),
            dma((GROUP,)),
            dma((3,)),
            dma((3,)),
            dma((3,)),
            dma((3,)),
            dma((4,)),
            dma((4,)),
        ],
        compiler_params=pltpu.CompilerParams(
            collective_id=0, has_side_effects=True, vmem_limit_bytes=LIMIT
        ),
        name="merge",
    )(clusters, frequency, perm, rows, sketch)


def exact_dot(left, right, dims):
    return lax.dot_general(
        left,
        right,
        (dims, ((), ())),
        precision=lax.Precision.HIGHEST,
        preferred_element_type=jnp.float32,
    )


def spread(value, row, column):
    size = value.shape[1]
    line = jnp.broadcast_to(value[row : row + 1, :], (8, size))
    return jnp.broadcast_to(line[:, column : column + 1], (8, size))


def inverse_factor(matrix):
    size = matrix.shape[0]
    count = size // 8
    groups = [matrix[g * 8 : g * 8 + 8, :] for g in range(count)]
    lane = lax.broadcasted_iota(jnp.int32, (8, size), 1)
    line = lax.broadcasted_iota(jnp.int32, (8, size), 0)
    out = []
    for g in range(count):
        base = g * 8
        inside = (lane >= base) & (lane < base + 8)
        pivot = [[spread(groups[g], r, base + s) for s in range(r + 1)] for r in range(8)]
        seeded = jnp.where(inside, jnp.where(lane == line + base, 1.0, 0.0), groups[g])
        rows = [jnp.broadcast_to(seeded[r : r + 1, :], (8, size)) for r in range(8)]
        inverses, factors = [], {}
        for s in range(8):
            inverse = 1.0 / pivot[s][s]
            inverses.append(inverse)
            for r in range(s + 1, 8):
                factors[r, s] = pivot[r][s] * inverse
            for r in range(s + 1, 8):
                for t in range(s + 1, r + 1):
                    pivot[r][t] = pivot[r][t] - factors[r, s] * pivot[t][s]
                rows[r] = rows[r] - factors[r, s] * rows[s]
        block = rows[7] * lax.rsqrt(pivot[7][7])
        for r in range(7):
            block = jnp.where(line == r, rows[r] * lax.rsqrt(pivot[r][r]), block)
        out.append(jnp.where(lane <= line + base, block, 0.0))
        if g == count - 1:
            break
        back = [None] * 8
        for s in reversed(range(8)):
            value = rows[s] * inverses[s]
            for r in reversed(range(s + 1, 8)):
                value = value - factors[r, s] * back[r]
            back[s] = value
        for h in range(g + 1, count):
            columns = [
                jnp.broadcast_to(groups[h][:, base + s : base + s + 1], (8, size))
                for s in range(8)
            ]
            value = jnp.where(inside, 0.0, groups[h])
            terms = [columns[s] * back[s] for s in range(8)]
            groups[h] = value - (
                ((terms[0] + terms[1]) + (terms[2] + terms[3]))
                + ((terms[4] + terms[5]) + (terms[6] + terms[7]))
            )
    return jnp.concatenate(out, axis=0)


def factor_kernel(full_ref, total_ref, merged_ref, out_ref, basis_ref, coef_ref, out_sem):
    out_copy = pltpu.make_async_copy(merged_ref, out_ref, out_sem)
    out_copy.start()
    ff, rank = full_ref.shape
    half = rank // 2
    turned = full_ref[...].astype(jnp.float32).T.astype(jnp.bfloat16)
    gram = jnp.dot(turned, full_ref[...], preferred_element_type=jnp.float32) / ff
    first = inverse_factor(gram[:half, :half])
    lower = exact_dot(gram[half:, :half], first, ((1,), (1,)))
    second = inverse_factor(gram[half:, half:] - exact_dot(lower, lower, ((1,), (1,))))
    corner = -exact_dot(second, exact_dot(lower, first, ((1,), (0,))), ((1,), (0,)))
    inverse = jnp.concatenate(
        [
            jnp.concatenate([first, jnp.zeros((half, half), jnp.float32)], axis=1),
            jnp.concatenate([corner, second], axis=1),
        ],
        axis=0,
    )
    turned_orth, rest = jnp.zeros((rank, ff), jnp.float32), inverse
    for _ in range(3):
        piece = rest.astype(jnp.bfloat16)
        rest = rest - piece.astype(jnp.float32)
        turned_orth = turned_orth + jnp.dot(piece, turned, preferred_element_type=jnp.float32)
    turned_orth = turned_orth.astype(jnp.bfloat16)
    coef_ref[...] = jnp.dot(
        turned_orth, merged_ref[...], preferred_element_type=jnp.float32
    ) * (1.0 / math.sqrt(ff))
    basis_ref[...] = exact_dot(total_ref[...], inverse, ((1,), (1,)))
    out_copy.wait()


def factor(full, total, merged):
    ff, rank = full.shape
    vmem = pl.BlockSpec(memory_space=pltpu.VMEM)
    return pl.pallas_call(
        factor_kernel,
        out_shape=(
            jax.ShapeDtypeStruct(merged.shape, merged.dtype),
            jax.ShapeDtypeStruct(total.shape, jnp.float32),
            jax.ShapeDtypeStruct((rank, merged.shape[1]), jnp.float32),
        ),
        in_specs=[vmem, vmem, vmem],
        out_specs=(pl.BlockSpec(memory_space=pl.ANY), vmem, vmem),
        scratch_shapes=[pltpu.SemaphoreType.DMA],
        compiler_params=pltpu.CompilerParams(vmem_limit_bytes=LIMIT),
        name="factor",
    )(full, total, merged)


def on_device(expert_rows, sketch, permutation, clusters, frequency):
    merged, full, total = merge(clusters, frequency, permutation, expert_rows[0], sketch)
    merged, basis, coef = factor(full, total, merged)
    return merged[None], basis[None], coef[None]


def solution(mesh):
    return jax.shard_map(
        on_device,
        mesh=mesh,
        in_specs=(P("expert", None, "shard"), P("shard", None), P("expert", None), P(), P()),
        out_specs=(
            P("expert", None, "shard"),
            P("expert", "shard", None),
            P("expert", None, "shard"),
        ),
        check_vma=False,
    )
```
